32 devices in a mesh: groups: 2 (over y), seq: 8 (over z, x), chan: 1, section: 2 (over core).
Axes of the slice: x: 2, y: 2, z: 4, core: 2. Of those that a mesh axis runs over, the one named last changes fastest.
Arguments:
- queries: bfloat16 [8192, 8192], P(('groups', 'seq', 'section'), 'chan'), parts along dimension 0, may hold values from -6 to 6
- key_proj: bfloat16 [8192, 8192], P(('groups', 'seq', 'section'), 'chan'), parts along dimension 0, may hold values from -6 to 6
- value_proj: bfloat16 [8192, 8192], P(('groups', 'seq', 'section'), 'chan'), parts along dimension 0, may hold values from -6 to 6
- filter_taps: bfloat16 [512, 128], P('chan'), may hold values from -0.5 to 0.5
- skip_gain: float32 [8192], P('chan'), may hold values from -3 to 3
- out_weight: bfloat16 [8192, 4096], P('chan', ('seq', 'section')), may hold values from -0.09375 to 0.09375
- residual: bfloat16 [8192, 4096], P(('groups', 'seq', 'section'), 'chan'), parts along dimension 0, may hold values from -6 to 6
Outputs:
- layer_out: bfloat16 [8192, 4096], P(('groups', 'seq', 'section'), 'chan'), parts along dimension 0
The draws below stay inside these ranges and needn't reach their ends.
There are 2 independent parts, one for each index of `groups`. The reference program is written for one: setup_inputs(seed, part) draws one part's arguments, and reference() takes and returns one part's arrays. A program takes and returns all parts, laid end to end along the dimension named above; an argument that names none is the same for every part. Nothing has to cross between parts.
All inputs are finite; a program needn't handle non-finite values.
Results may differ from the reference program's by a relative error of at most 0.0053.
Values may be sent and summed in bfloat16 or wider, within the bound.
A program may use at most 256 MiB of HBM per device.

```python
import jax
import jax.numpy as jnp
from jax import lax

C = 8192
OUT = 4096
GROUPS = 512
BLOCK = 128
TOKENS = 4096


def with_spikes(result, stream_key, source, target, blocks, factor):
    def block_of(dim):
        return (jnp.arange(result.shape[dim]) // (result.shape[dim] // blocks)).reshape((-1,) + (1,) * (result.ndim - 1 - dim))

    first = jax.random.permutation(stream_key, blocks)[block_of(target)]
    other_side = (block_of(target) + blocks // 2) % blocks
    return jnp.where((block_of(source) == first) | (block_of(source) == other_side), factor * result, result)


def shard_levels(rng, shape, pieces, smallest, high):
    def one(position, shards_of):
        heights = jax.random.uniform(jax.random.fold_in(jax.random.fold_in(rng, 6), position), (shards_of,), jnp.float32, smallest / len(pieces), high / len(pieces))
        return jnp.repeat(jnp.exp(heights), shape[position] // shards_of).reshape((-1,) + (1,) * (len(shape) - position - 1))

    factor_of = one(*pieces[0])
    for cut in pieces[1:]:
        factor_of = factor_of * one(*cut)
    return factor_of


def gaussian(stream_key, extent, deviation, reach, cuts=(), dtype=jnp.bfloat16):
    result = deviation * jax.random.normal(stream_key, extent, jnp.float32)
    if cuts:
        result = result * shard_levels(stream_key, extent, cuts, -0.22, 0.18)
    return jnp.clip(result, -reach, reach).astype(dtype)


def heavy_noise(rng, dims, deviation, bound, cuts, heavy, dtype=jnp.bfloat16):
    drawn = deviation * jax.random.normal(rng, dims, jnp.float32)
    if cuts:
        drawn = drawn * shard_levels(rng, dims, cuts, -0.22, 0.18)
    return jnp.clip(with_spikes(drawn, jax.random.fold_in(rng, 3), *heavy), -bound, bound).astype(dtype)


def setup_inputs(seed: int = 0, part: int = 0) -> dict:
    splits = jax.random.split(jax.random.key(seed), 8)
    own_keys = jax.random.split(jax.random.fold_in(splits[7], part), 8)
    return {
        "queries": gaussian(own_keys[0], (TOKENS, C), 1.0, 6.0, ((0, 16),)),
        "key_proj": gaussian(own_keys[1], (TOKENS, C), 1.0, 6.0, ((0, 16),)),
        "value_proj": gaussian(own_keys[2], (TOKENS, C), 1.0, 6.0, ((0, 16),)),
        "filter_taps": gaussian(splits[3], (GROUPS, BLOCK), BLOCK ** -0.5, 0.5),
        "skip_gain": gaussian(splits[4], (C,), 0.5, 3.0, (), jnp.float32),
        "out_weight": heavy_noise(splits[5], (C, OUT), C ** -0.5, 0.09375, ((1, 16),), (0, 1, 16, 2.0)),
        "residual": gaussian(own_keys[6], (TOKENS, OUT), 1.0, 6.0, ((0, 16),)),
    }


def reference(queries, key_proj, value_proj, filter_taps, skip_gain, out_weight, residual):
    product = (key_proj.astype(jnp.float32) * value_proj.astype(jnp.float32)).astype(jnp.bfloat16)
    product_f = product.astype(jnp.float32)
    channel_taps = jnp.repeat(filter_taps.astype(jnp.float32), C // GROUPS, axis=0)
    padded = jnp.pad(product_f, ((BLOCK - 1, 0), (0, 0)))

    def add_tap(offset, convolved):
        start = (BLOCK - 1 - jnp.asarray(offset)).astype(jnp.int32)
        shifted = lax.dynamic_slice_in_dim(padded, start, TOKENS, 0)
        column = lax.dynamic_slice_in_dim(channel_taps, jnp.asarray(offset).astype(jnp.int32), 1, 1)[:, 0]
        return convolved + shifted * column[None, :]

    convolved = lax.fori_loop(0, BLOCK, add_tap, jnp.zeros((TOKENS, C), jnp.float32))
    gated = (queries.astype(jnp.float32) * (convolved + skip_gain[None, :] * product_f)).astype(jnp.bfloat16)
    projected = jnp.dot(gated, out_weight, preferred_element_type=jnp.float32)
    return (residual.astype(jnp.float32) + projected).astype(jnp.bfloat16)
```

```python
import functools

import jax
import jax.numpy as jnp
from jax import lax
from jax.experimental import pallas as pl
from jax.experimental.pallas import tpu as pltpu
from jax.sharding import PartitionSpec as P


def shifted(value, axis, steps):
    count = lax.axis_size(axis)
    initial, last = (max(0, -steps), min(count, count - steps))
    return lax.ppermute(value, axis, [(source, source + steps) for source in range(initial, last)])


def filter_matrices(filter_taps):
    groups_here, block_len = filter_taps.shape
    pattern = jnp.concatenate(
        [
            jnp.zeros((groups_here, 1), filter_taps.dtype),
            filter_taps[:, ::-1],
            jnp.zeros((groups_here, block_len), filter_taps.dtype),
        ],
        axis=1,
    )
    tiled = jnp.tile(pattern, (1, block_len))[:, : block_len * 2 * block_len]
    both = tiled.reshape(groups_here, block_len, 2 * block_len)
    return (both[:, :, block_len:], both[:, :, :block_len])


def apply_blocks(matrix, blocks):
    return jnp.einsum("gij,bjgc->bigc", matrix, blocks, preferred_element_type=jnp.float32)


def body(queries, key_proj, value_proj, filter_taps, skip_gain, out_weight, residual):
    seq_len, channels = queries.shape
    groups_here, block_len = filter_taps.shape
    per_group = channels // groups_here
    block_count = seq_len // block_len
    product = (key_proj.astype(jnp.float32) * value_proj.astype(jnp.float32)).astype(jnp.bfloat16)
    blocks = product.reshape(block_count, block_len, groups_here, per_group)
    now_matrix, prev_matrix = filter_matrices(filter_taps)
    convolved = apply_blocks(now_matrix, blocks)
    carried = apply_blocks(prev_matrix, blocks)
    outgoing = carried[block_count - 1, : block_len - 1].reshape(block_len - 1, channels)
    incoming = shifted(outgoing, ("seq", "section"), 1)
    first = jnp.concatenate([incoming, jnp.zeros((1, channels), jnp.float32)], axis=0)
    first = first.reshape(1, block_len, groups_here, per_group)
    carried = jnp.concatenate([first, carried[: block_count - 1]], axis=0)
    convolved = (convolved + carried).reshape(seq_len, channels)
    gated = (
        queries.astype(jnp.float32) * (convolved + skip_gain[None, :] * product.astype(jnp.float32))
    ).astype(jnp.bfloat16)
    partial_out = jnp.dot(
        gated,
        lax.all_gather(out_weight, ("seq", "section"), axis=1, tiled=True),
        preferred_element_type=jnp.float32,
    )
    out_share = lax.psum_scatter(partial_out, "chan", scatter_dimension=1, tiled=True)
    return (residual.astype(jnp.float32) + out_share).astype(jnp.bfloat16)


LANES = 128
PIECES = 4


def mixer_kernel(
    seq_count, per_group,
    q_hbm, k_hbm, v_hbm, pattern_ref, skip_ref, w_hbm,
    g_full, w_full,
    q_buf, k_buf, v_buf, gated, tail, halo,
    load_sem, local_sem, halo_sem, zsend, zrecv, ysend, yrecv, xsend, xrecv, csend, crecv, fsend, frecv,
):
    group, seq, chan, core = (lax.axis_index(a) for a in ("groups", "seq", "chan", "section"))
    far, near = seq // 2, seq % 2
    line = seq_count // 2
    rows, channels = q_hbm.shape
    depth, width = w_hbm.shape
    block = tail.shape[0]
    half = depth // 2
    piece = half // PIECES
    chunk = channels // PIECES
    me = near * 2 + core

    def place(s, c, g=group):
        return (g, s, chan, c)

    core_mate = place(seq, 1 - core)
    near_mate = place(far * 2 + 1 - near, core)
    group_mate = place(seq, core, 1 - group)
    linear = seq * 2 + core
    after = lax.rem(linear + 1, seq_count * 2)
    before = lax.rem(linear + seq_count * 2 - 1, seq_count * 2)
    after, before = place(after // 2, after % 2), place(before // 2, before % 2)

    loads = [
        pltpu.make_async_copy(src, dst, load_sem.at[i])
        for i, (src, dst) in enumerate(((k_hbm, k_buf), (v_hbm, v_buf), (q_hbm, q_buf)))
    ]
    for load in loads:
        load.start()
    own_cols = pl.ds(pl.multiple_of(far * width, width), width)
    keep = pltpu.make_async_copy(w_hbm, w_full.at[:, own_cols], local_sem.at[0])
    keep.start()

    barrier = pltpu.get_barrier_semaphore()
    peers = [place(lax.rem(far + d, line) * 2 + near, core) for d in range(1, line)]
    for peer in peers + [core_mate, near_mate, group_mate, after, before]:
        pl.semaphore_signal(barrier, inc=1, device_id=peer, device_id_type=pl.DeviceIdType.MESH)
    pl.semaphore_wait(barrier, len(peers) + 5)

    def remote(src, dst, send, recv, device):
        return pltpu.make_async_remote_copy(
            src_ref=src, dst_ref=dst, send_sem=send, recv_sem=recv,
            device_id=device, device_id_type=pl.DeviceIdType.MESH,
        )

    def span(which, p):
        return pl.ds(pl.multiple_of(which * half + p * piece, piece), piece)

    def cols(z):
        return pl.ds(pl.multiple_of(z * width, width), width)

    loads[0].wait()
    loads[1].wait()
    tail[...] = (
        k_buf[rows - block :, :].astype(jnp.float32) * v_buf[rows - block :, :].astype(jnp.float32)
    ).astype(jnp.bfloat16)
    edge = remote(tail, halo, halo_sem.at[0], halo_sem.at[1], after)
    edge.start()

    def along(d, p):
        return remote(
            w_hbm.at[span(group, p), :], w_full.at[span(group, p), cols(far)],
            zsend.at[d - 1, p], zrecv.at[d - 1, p], peers[d - 1],
        )

    def across(d, p, which):
        part = w_full.at[span(which, p), cols(lax.rem(far + line - d, line))]
        return remote(part, part, ysend.at[d - 1, p], yrecv.at[d - 1, p], group_mate)

    for p in range(PIECES):
        for d in range(1, line):
            along(d, p).start()

    loads[2].wait()
    edge.wait()

    groups_per_tile = LANES // per_group
    lane_group = lax.broadcasted_iota(jnp.int32, (block, 2 * LANES), 1) % LANES // per_group
    first = linear == 0

    def tile(t, carry):
        lanes = pl.ds(pl.multiple_of(t * LANES, LANES), LANES)
        product = (k_buf[:, lanes].astype(jnp.float32) * v_buf[:, lanes].astype(jnp.float32)).astype(jnp.bfloat16)
        past = halo[:, lanes]
        past = jnp.where(first, jnp.zeros_like(past), past)
        upper, lower = product[:block], product[block:]
        window = jnp.concatenate(
            [jnp.concatenate([past, upper], axis=1), jnp.concatenate([upper, lower], axis=1)], axis=0
        )
        taps = pattern_ref[pl.ds(pl.multiple_of(t * groups_per_tile, groups_per_tile), groups_per_tile), :]
        matrices = []
        for g in range(groups_per_tile):
            row = jnp.broadcast_to(taps[g : g + 1, :], (block, 2 * block))
            matrices.append(pltpu.roll(row, 0, 1, stride=1, stride_axis=0).astype(jnp.bfloat16))
        every = jnp.dot(jnp.concatenate(matrices, axis=0), window, preferred_element_type=jnp.float32)
        total = every[:block]
        for g in range(1, groups_per_tile):
            total = jnp.where(lane_group == g, every[g * block : (g + 1) * block], total)
        convolved = jnp.concatenate([total[:, :LANES], total[:, LANES:]], axis=0)
        gated[:, lanes] = (
            q_buf[:, lanes].astype(jnp.float32)
            * (convolved + skip_ref[:, lanes] * product.astype(jnp.float32))
        ).astype(jnp.bfloat16)
        return carry

    def slot(index, j):
        return g_full.at[pl.ds(pl.multiple_of(index * rows, rows), rows), j * chunk : (j + 1) * chunk]

    def to_near(j):
        return remote(gated.at[:, j * chunk : (j + 1) * chunk], slot(me, j), xsend.at[j], xrecv.at[j], near_mate)

    def to_core(j):
        return remote(gated.at[:, j * chunk : (j + 1) * chunk], slot(me, j), csend.at[j], crecv.at[j], core_mate)

    def pass_on(j):
        part = slot((1 - near) * 2 + core, j)
        return remote(part, part, fsend.at[j], frecv.at[j], core_mate)

    tiles = chunk // LANES
    for j in range(PIECES):
        lax.fori_loop(j * tiles, (j + 1) * tiles, tile, 0)
        to_near(j).start()
        to_core(j).start()
    mine = pltpu.make_async_copy(gated, g_full.at[pl.ds(pl.multiple_of(me * rows, rows), rows), :], local_sem.at[1])
    mine.start()

    for p in range(PIECES):
        to_near(p).wait_recv()
        pass_on(p).start()
        for d in range(1, line):
            along(d, p).wait_recv()
            across(d, p, group).start()
    keep.wait()
    mine.wait()
    for p in range(PIECES):
        to_near(p).wait_send()
        to_core(p).wait()
        pass_on(p).wait()
        for d in range(1, line):
            along(d, p).wait_send()
            across(d, p, group).wait()


def tiled_body(mesh, queries, key_proj, value_proj, filter_taps, skip_gain, out_weight, residual):
    rows, channels = queries.shape
    groups_here, block = filter_taps.shape
    depth, width = out_weight.shape
    seq_count = mesh.shape["seq"]
    line = seq_count // 2
    pattern = jnp.pad(filter_taps.astype(jnp.float32)[:, ::-1], ((0, 0), (1, block - 1)))
    hbm = pl.BlockSpec(memory_space=pl.ANY)
    vmem = pl.BlockSpec(memory_space=pltpu.VMEM)
    dma = pltpu.SemaphoreType.DMA
    bf16 = jnp.bfloat16
    g_full, w_full = pl.pallas_call(
        functools.partial(mixer_kernel, seq_count, channels // groups_here),
        out_shape=(
            jax.ShapeDtypeStruct((4 * rows, channels), bf16),
            jax.ShapeDtypeStruct((depth, line * width), bf16),
        ),
        in_specs=[hbm, hbm, hbm, vmem, vmem, hbm],
        out_specs=(hbm, hbm),
        scratch_shapes=[pltpu.VMEM((rows, channels), bf16)] * 4
        + [pltpu.VMEM((block, channels), bf16)] * 2
        + [dma((3,)), dma((2,)), dma((2,))]
        + [dma((line - 1, PIECES))] * 4
        + [dma((PIECES,))] * 6,
        compiler_params=pltpu.CompilerParams(
            collective_id=0, has_side_effects=True, vmem_limit_bytes=48 * 2**20
        ),
    )(queries, key_proj, value_proj, pattern, skip_gain[None, :], out_weight)
    out = jnp.dot(g_full, w_full, preferred_element_type=jnp.float32).astype(bf16)
    seq, core = lax.axis_index("seq"), lax.axis_index("section")
    me = (seq % 2) * 2 + core
    pieces = []
    for m in range(4):
        part = lax.dynamic_slice_in_dim(out, jnp.bitwise_xor(me, m) * rows, rows, 0)
        if m:
            part = lax.ppermute(part, ("seq", "section"), [(i, i ^ m) for i in range(seq_count * 2)])
        pieces.append(part.reshape(rows, line, width))
    columns = []
    for target in range(4):
        m = jnp.bitwise_xor(me, target)
        columns.append(jnp.where(m < 2, jnp.where(m == 0, pieces[0], pieces[1]), jnp.where(m == 2, pieces[2], pieces[3])))
    projected = jnp.stack(columns, axis=2).reshape(rows, line * 4 * width)
    return (residual.astype(jnp.float32) + projected.astype(jnp.float32)).astype(bf16)


def choose(mesh, *args):
    rows, channels = args[0].shape
    groups_here, block = args[3].shape
    if (
        mesh.shape["chan"] == 1 and mesh.shape["groups"] == 2 and mesh.shape["section"] == 2
        and mesh.shape["seq"] % 2 == 0 and mesh.shape["seq"] >= 4
        and block == LANES and rows == 2 * block and channels // groups_here * 8 == LANES
    ):
        return tiled_body(mesh, *args)
    return body(*args)


def solution(mesh):
    return jax.shard_map(
        functools.partial(choose, mesh),
        mesh=mesh,
        in_specs=(
            P(("groups", "seq", "section"), "chan"),
            P(("groups", "seq", "section"), "chan"),
            P(("groups", "seq", "section"), "chan"),
            P("chan", None),
            P("chan"),
            P("chan", ("seq", "section")),
            P(("groups", "seq", "section"), "chan"),
        ),
        out_specs=P(("groups", "seq", "section"), "chan"),
        check_vma=False,
    )
```

```python
import functools

import jax
import jax.numpy as jnp
from jax import lax
from jax.experimental import pallas as pl
from jax.experimental.pallas import tpu as pltpu
from jax.sharding import PartitionSpec as P


def shifted(value, axis, steps):
    count = lax.axis_size(axis)
    initial, last = (max(0, -steps), min(count, count - steps))
    return lax.ppermute(value, axis, [(source, source + steps) for source in range(initial, last)])


def filter_matrices(filter_taps):
    groups_here, block_len = filter_taps.shape
    pattern = jnp.concatenate(
        [
            jnp.zeros((groups_here, 1), filter_taps.dtype),
            filter_taps[:, ::-1],
            jnp.zeros((groups_here, block_len), filter_taps.dtype),
        ],
        axis=1,
    )
    tiled = jnp.tile(pattern, (1, block_len))[:, : block_len * 2 * block_len]
    both = tiled.reshape(groups_here, block_len, 2 * block_len)
    return (both[:, :, block_len:], both[:, :, :block_len])


def apply_blocks(matrix, blocks):
    return jnp.einsum("gij,bjgc->bigc", matrix, blocks, preferred_element_type=jnp.float32)


def body(queries, key_proj, value_proj, filter_taps, skip_gain, out_weight, residual):
    seq_len, channels = queries.shape
    groups_here, block_len = filter_taps.shape
    per_group = channels // groups_here
    block_count = seq_len // block_len
    product = (key_proj.astype(jnp.float32) * value_proj.astype(jnp.float32)).astype(jnp.bfloat16)
    blocks = product.reshape(block_count, block_len, groups_here, per_group)
    now_matrix, prev_matrix = filter_matrices(filter_taps)
    convolved = apply_blocks(now_matrix, blocks)
    carried = apply_blocks(prev_matrix, blocks)
    outgoing = carried[block_count - 1, : block_len - 1].reshape(block_len - 1, channels)
    incoming = shifted(outgoing, ("seq", "section"), 1)
    first = jnp.concatenate([incoming, jnp.zeros((1, channels), jnp.float32)], axis=0)
    first = first.reshape(1, block_len, groups_here, per_group)
    carried = jnp.concatenate([first, carried[: block_count - 1]], axis=0)
    convolved = (convolved + carried).reshape(seq_len, channels)
    gated = (
        queries.astype(jnp.float32) * (convolved + skip_gain[None, :] * product.astype(jnp.float32))
    ).astype(jnp.bfloat16)
    partial_out = jnp.dot(
        gated,
        lax.all_gather(out_weight, ("seq", "section"), axis=1, tiled=True),
        preferred_element_type=jnp.float32,
    )
    out_share = lax.psum_scatter(partial_out, "chan", scatter_dimension=1, tiled=True)
    return (residual.astype(jnp.float32) + out_share).astype(jnp.bfloat16)


LANES = 128
PIECES = 4


def mixer_kernel(
    seq_count, per_group,
    q_hbm, k_hbm, v_hbm, pattern_ref, skip_ref, w_hbm, res_ref,
    out_ref, w_full,
    q_buf, k_buf, v_buf, g_buf, tail, halo, total_buf, w_buf, leaving, arriving,
    load_sem, local_sem, halo_sem, hsend, zsend, zrecv, ysend, yrecv, xsend, xrecv, csend, crecv, fsend, frecv, osend, orecv,
):
    group, seq, chan, core = (lax.axis_index(a) for a in ("groups", "seq", "chan", "section"))
    far, near = seq // 2, seq % 2
    line = seq_count // 2
    rows, channels = q_hbm.shape
    depth, width = w_hbm.shape
    block = tail.shape[0]
    half = depth // 2
    piece = half // PIECES
    chunk = channels // PIECES
    me = near * 2 + core

    def place(s, c, g=group):
        return (g, s, chan, c)

    core_mate = place(seq, 1 - core)
    near_mate = place(far * 2 + 1 - near, core)
    group_mate = place(seq, core, 1 - group)
    linear = seq * 2 + core
    after = lax.rem(linear + 1, seq_count * 2)
    before = lax.rem(linear + seq_count * 2 - 1, seq_count * 2)
    after, before = place(after // 2, after % 2), place(before // 2, before % 2)

    loads = [
        pltpu.make_async_copy(src, dst, load_sem.at[i])
        for i, (src, dst) in enumerate(((k_hbm, k_buf), (v_hbm, v_buf), (q_hbm, q_buf)))
    ]
    for load in loads:
        load.start()
    own_cols = pl.ds(pl.multiple_of(far * width, width), width)
    keep = pltpu.make_async_copy(w_hbm, w_full.at[:, own_cols], local_sem.at[0])
    keep.start()

    barrier = pltpu.get_barrier_semaphore()
    peers = [place(lax.rem(far + d, line) * 2 + near, core) for d in range(1, line)]
    for peer in peers + [core_mate, near_mate, group_mate, after, before]:
        pl.semaphore_signal(barrier, inc=1, device_id=peer, device_id_type=pl.DeviceIdType.MESH)
    pl.semaphore_wait(barrier, len(peers) + 5)

    def remote(src, dst, send, recv, device):
        return pltpu.make_async_remote_copy(
            src_ref=src, dst_ref=dst, send_sem=send, recv_sem=recv,
            device_id=device, device_id_type=pl.DeviceIdType.MESH,
        )

    def span(which, p):
        return pl.ds(pl.multiple_of(which * half + p * piece, piece), piece)

    def cols(z):
        return pl.ds(pl.multiple_of(z * width, width), width)

    loads[0].wait()
    loads[1].wait()
    tail[...] = (
        k_buf[rows - block :, :].astype(jnp.float32) * v_buf[rows - block :, :].astype(jnp.float32)
    ).astype(jnp.bfloat16)
    edge = remote(tail, halo, halo_sem.at[0], halo_sem.at[1], after)
    edge.start()

    def source(d):
        return lax.rem(far + line - d, line)

    def along_z(src, dst, send, d, p, step):
        return remote(src, dst, send, zrecv.at[d - 1, p], place((far + step) * 2 + near, core))

    def own_right(p):
        return along_z(w_hbm.at[span(group, p), :], w_full.at[span(group, p), cols(far)], hsend.at[0, p], 1, p, 1)

    def own_left(p):
        return along_z(w_hbm.at[span(group, p), :], w_full.at[span(group, p), cols(far)], hsend.at[1, p], line - 1, p, -1)

    def onward(d, p, step):
        part = w_full.at[span(group, p), cols(source(d))]
        return along_z(part, part, zsend.at[d - 1, p], d + step, p, step)

    def across(d, p, which):
        part = w_full.at[span(which, p), cols(source(d))]
        return remote(part, part, ysend.at[d - 1, p], yrecv.at[d - 1, p], group_mate)

    order = [sorted(range(1, line), key=lambda d, z=z: d if d <= z else line - d) for z in range(line)]

    def nth(k):
        return sum((far == z).astype(jnp.int32) * order[z][k] for z in range(line))

    def goes_right(d):
        return (far >= d) & (far < line - 1)

    def goes_left(d):
        return (far < d) & (far > 0)

    def hand_on(k, p):
        d = nth(k)
        part = w_full.at[span(group, p), cols(source(d))]
        remote(part, part, zsend.at[d - 1, p], zrecv.at[d - 1, p], group_mate).wait_recv()

        @pl.when(goes_right(d))
        def _():
            onward(d, p, 1).start()

        @pl.when(goes_left(d))
        def _():
            onward(d, p, -1).start()

        across(d, p, group).start()

    for p in range(PIECES):
        @pl.when(far < line - 1)
        def _():
            own_right(p).start()

        @pl.when(far > 0)
        def _():
            own_left(p).start()

    loads[2].wait()
    edge.wait()

    groups_per_tile = LANES // per_group
    lane_group = lax.broadcasted_iota(jnp.int32, (block, 2 * LANES), 1) % LANES // per_group
    first = linear == 0
    my_rows = pl.ds(pl.multiple_of(me * rows, rows), rows)
    total_buf[...] = jnp.zeros_like(total_buf)

    def tile(t, carry):
        lanes = pl.ds(pl.multiple_of(t * LANES, LANES), LANES)
        product = (k_buf[:, lanes].astype(jnp.float32) * v_buf[:, lanes].astype(jnp.float32)).astype(jnp.bfloat16)
        past = halo[:, lanes]
        past = jnp.where(first, jnp.zeros_like(past), past)
        upper, lower = product[:block], product[block:]
        window = jnp.concatenate(
            [jnp.concatenate([past, upper], axis=1), jnp.concatenate([upper, lower], axis=1)], axis=0
        )
        taps = pattern_ref[pl.ds(pl.multiple_of(t * groups_per_tile, groups_per_tile), groups_per_tile), :]
        matrices = []
        for g in range(groups_per_tile):
            row = jnp.broadcast_to(taps[g : g + 1, :], (block, 2 * block))
            matrices.append(pltpu.roll(row, 0, 1, stride=1, stride_axis=0).astype(jnp.bfloat16))
        every = jnp.dot(jnp.concatenate(matrices, axis=0), window, preferred_element_type=jnp.float32)
        total = every[:block]
        for g in range(1, groups_per_tile):
            total = jnp.where(lane_group == g, every[g * block : (g + 1) * block], total)
        convolved = jnp.concatenate([total[:, :LANES], total[:, LANES:]], axis=0)
        g_buf[my_rows, lanes] = (
            q_buf[:, lanes].astype(jnp.float32)
            * (convolved + skip_ref[:, lanes] * product.astype(jnp.float32))
        ).astype(jnp.bfloat16)
        return carry

    def slot(index, j):
        return g_buf.at[pl.ds(pl.multiple_of(index * rows, rows), rows), j * chunk : (j + 1) * chunk]

    def to_near(j):
        return remote(slot(me, j), slot(me, j), xsend.at[j], xrecv.at[j], near_mate)

    def to_core(j):
        return remote(slot(me, j), slot(me, j), csend.at[j], crecv.at[j], core_mate)

    def pass_on(j):
        part = slot((1 - near) * 2 + core, j)
        return remote(part, part, fsend.at[j], frecv.at[j], core_mate)

    tiles = chunk // LANES
    for j in range(PIECES):
        lax.fori_loop(j * tiles, (j + 1) * tiles, tile, 0)
        to_near(j).start()
        to_core(j).start()
        if j == PIECES - 2:
            for p in range(PIECES // 2):
                hand_on(0, p)
    for p in range(PIECES // 2, PIECES):
        hand_on(0, p)

    def relay(j):
        to_near(j).wait_recv()
        pass_on(j).start()

    for p in range(PIECES):
        relay(p)
        for k in range(1, line - 2):
            hand_on(k, p)
    keep.wait()

    def multiply(which, p):
        load = pltpu.make_async_copy(w_full.at[span(which, p), :], w_buf, local_sem.at[1])
        load.start()
        load.wait()

        def rows_of(r, carry):
            at = pl.ds(pl.multiple_of(r * rows, rows), rows)
            total_buf[at, :] += jnp.dot(g_buf[at, span(which, p)], w_buf[...], preferred_element_type=jnp.float32)
            return carry

        lax.fori_loop(0, 4, rows_of, 0)

    def from_mate(p):
        for d in range(1, line):
            across(d, p, 1 - group).wait_recv()
        multiply(1 - group, p)

    for p in range(PIECES):
        hand_on(line - 2, p)
        if p == 0:
            for j in range(PIECES):
                to_core(j).wait_recv()
                pass_on(j).wait_recv()
        multiply(group, p)
        if p:
            from_mate(p - 1)
    from_mate(PIECES - 1)

    def other(m):
        return (1 - near if m >= 2 else near), (1 - core if m % 2 else core)

    def give(m):
        n, c = other(m)
        return remote(leaving.at[m - 1], arriving.at[m - 1], osend.at[m - 1], orecv.at[m - 1], place(far * 2 + n, c))

    for m in (3, 2, 1):
        n, c = other(m)
        at = pl.ds(pl.multiple_of((n * 2 + c) * rows, rows), rows)
        leaving[m - 1] = total_buf[at, :].astype(jnp.bfloat16)
        give(m).start()

    for m in (0, 1, 2, 3):
        n, c = other(m)
        if m:
            give(m).wait()
        for z in range(line):
            at = pl.ds(pl.multiple_of((z * 4 + n * 2 + c) * width, width), width)
            here = slice(z * width, (z + 1) * width)
            part = arriving[m - 1, :, here].astype(jnp.float32) if m else total_buf[my_rows, here]
            out_ref[:, at] = (res_ref[:, at].astype(jnp.float32) + part).astype(jnp.bfloat16)

    for p in range(PIECES):
        to_near(p).wait_send()
        to_core(p).wait_send()
        pass_on(p).wait_send()

        @pl.when(far < line - 1)
        def _():
            own_right(p).wait_send()

        @pl.when(far > 0)
        def _():
            own_left(p).wait_send()

        for d in range(1, line):
            @pl.when(goes_right(d) | goes_left(d))
            def _():
                part = w_full.at[span(group, p), cols(source(d))]
                remote(part, part, zsend.at[d - 1, p], zrecv.at[d - 1, p], group_mate).wait_send()

            across(d, p, group).wait_send()


def tiled_body(mesh, queries, key_proj, value_proj, filter_taps, skip_gain, out_weight, residual):
    rows, channels = queries.shape
    groups_here, block = filter_taps.shape
    depth, width = out_weight.shape
    seq_count = mesh.shape["seq"]
    line = seq_count // 2
    pattern = jnp.pad(filter_taps.astype(jnp.float32)[:, ::-1], ((0, 0), (1, block - 1)))
    hbm = pl.BlockSpec(memory_space=pl.ANY)
    vmem = pl.BlockSpec(memory_space=pltpu.VMEM)
    dma = pltpu.SemaphoreType.DMA
    bf16 = jnp.bfloat16
    out, _ = pl.pallas_call(
        functools.partial(mixer_kernel, seq_count, channels // groups_here),
        out_shape=(
            jax.ShapeDtypeStruct(residual.shape, bf16),
            jax.ShapeDtypeStruct((depth, line * width), bf16),
        ),
        in_specs=[hbm, hbm, hbm, vmem, vmem, hbm, vmem],
        out_specs=(vmem, hbm),
        scratch_shapes=[pltpu.VMEM((rows, channels), bf16)] * 3
        + [pltpu.VMEM((4 * rows, channels), bf16)]
        + [pltpu.VMEM((block, channels), bf16)] * 2
        + [pltpu.VMEM((4 * rows, line * width), jnp.float32), pltpu.VMEM((depth // (2 * PIECES), line * width), bf16)]
        + [pltpu.VMEM((3, rows, line * width), bf16)] * 2
        + [dma((3,)), dma((2,)), dma((2,)), dma((2, PIECES))]
        + [dma((line - 1, PIECES))] * 4
        + [dma((PIECES,))] * 6
        + [dma((3,))] * 2,
        compiler_params=pltpu.CompilerParams(
            collective_id=0, has_side_effects=True, vmem_limit_bytes=60 * 2**20
        ),
    )(queries, key_proj, value_proj, pattern, skip_gain[None, :], out_weight, residual)
    return out


def choose(mesh, *args):
    rows, channels = args[0].shape
    groups_here, block = args[3].shape
    if (
        mesh.shape["chan"] == 1 and mesh.shape["groups"] == 2 and mesh.shape["section"] == 2
        and mesh.shape["seq"] % 2 == 0 and mesh.shape["seq"] >= 6
        and block == LANES and rows == 2 * block and channels // groups_here * 8 == LANES
    ):
        return tiled_body(mesh, *args)
    return body(*args)


def solution(mesh):
    return jax.shard_map(
        functools.partial(choose, mesh),
        mesh=mesh,
        in_specs=(
            P(("groups", "seq", "section"), "chan"),
            P(("groups", "seq", "section"), "chan"),
            P(("groups", "seq", "section"), "chan"),
            P("chan", None),
            P("chan"),
            P("chan", ("seq", "section")),
            P(("groups", "seq", "section"), "chan"),
        ),
        out_specs=P(("groups", "seq", "section"), "chan"),
        check_vma=False,
    )
```

```python
import functools

import jax
import jax.numpy as jnp
from jax import lax
from jax.experimental import pallas as pl
from jax.experimental.pallas import tpu as pltpu
from jax.sharding import PartitionSpec as P


def shifted(value, axis, steps):
    count = lax.axis_size(axis)
    initial, last = (max(0, -steps), min(count, count - steps))
    return lax.ppermute(value, axis, [(source, source + steps) for source in range(initial, last)])


def filter_matrices(filter_taps):
    groups_here, block_len = filter_taps.shape
    pattern = jnp.concatenate(
        [
            jnp.zeros((groups_here, 1), filter_taps.dtype),
            filter_taps[:, ::-1],
            jnp.zeros((groups_here, block_len), filter_taps.dtype),
        ],
        axis=1,
    )
    tiled = jnp.tile(pattern, (1, block_len))[:, : block_len * 2 * block_len]
    both = tiled.reshape(groups_here, block_len, 2 * block_len)
    return (both[:, :, block_len:], both[:, :, :block_len])


def apply_blocks(matrix, blocks):
    return jnp.einsum("gij,bjgc->bigc", matrix, blocks, preferred_element_type=jnp.float32)


def body(queries, key_proj, value_proj, filter_taps, skip_gain, out_weight, residual):
    seq_len, channels = queries.shape
    groups_here, block_len = filter_taps.shape
    per_group = channels // groups_here
    block_count = seq_len // block_len
    product = (key_proj.astype(jnp.float32) * value_proj.astype(jnp.float32)).astype(jnp.bfloat16)
    blocks = product.reshape(block_count, block_len, groups_here, per_group)
    now_matrix, prev_matrix = filter_matrices(filter_taps)
    convolved = apply_blocks(now_matrix, blocks)
    carried = apply_blocks(prev_matrix, blocks)
    outgoing = carried[block_count - 1, : block_len - 1].reshape(block_len - 1, channels)
    incoming = shifted(outgoing, ("seq", "section"), 1)
    first = jnp.concatenate([incoming, jnp.zeros((1, channels), jnp.float32)], axis=0)
    first = first.reshape(1, block_len, groups_here, per_group)
    carried = jnp.concatenate([first, carried[: block_count - 1]], axis=0)
    convolved = (convolved + carried).reshape(seq_len, channels)
    gated = (
        queries.astype(jnp.float32) * (convolved + skip_gain[None, :] * product.astype(jnp.float32))
    ).astype(jnp.bfloat16)
    partial_out = jnp.dot(
        gated,
        lax.all_gather(out_weight, ("seq", "section"), axis=1, tiled=True),
        preferred_element_type=jnp.float32,
    )
    out_share = lax.psum_scatter(partial_out, "chan", scatter_dimension=1, tiled=True)
    return (residual.astype(jnp.float32) + out_share).astype(jnp.bfloat16)


LANES = 128
PIECES = 8


def mixer_kernel(
    seq_count, per_group,
    q_hbm, k_hbm, v_hbm, pattern_ref, skip_ref, w_hbm, res_ref,
    out_ref, w_full,
    q_buf, k_buf, v_buf, g_buf, tail, halo, total_buf, w_buf, leaving, arriving,
    load_sem, local_sem, halo_sem, hsend, zsend, zrecv, ysend, yrecv, xsend, xrecv, csend, crecv, fsend, frecv, osend, orecv,
):
    group, seq, chan, core = (lax.axis_index(a) for a in ("groups", "seq", "chan", "section"))
    far, near = seq // 2, seq % 2
    line = seq_count // 2
    rows, channels = q_hbm.shape
    depth, width = w_hbm.shape
    block = tail.shape[0]
    half = depth // 2
    piece = half // PIECES
    chunk = channels // PIECES
    me = near * 2 + core

    def place(s, c, g=group):
        return (g, s, chan, c)

    core_mate = place(seq, 1 - core)
    near_mate = place(far * 2 + 1 - near, core)
    group_mate = place(seq, core, 1 - group)
    linear = seq * 2 + core
    after = lax.rem(linear + 1, seq_count * 2)
    before = lax.rem(linear + seq_count * 2 - 1, seq_count * 2)
    after, before = place(after // 2, after % 2), place(before // 2, before % 2)

    loads = [
        pltpu.make_async_copy(src, dst, load_sem.at[i])
        for i, (src, dst) in enumerate(((k_hbm, k_buf), (v_hbm, v_buf), (q_hbm, q_buf)))
    ]
    for load in loads:
        load.start()
    own_cols = pl.ds(pl.multiple_of(far * width, width), width)
    keep = pltpu.make_async_copy(w_hbm, w_full.at[:, own_cols], local_sem.at[0])
    keep.start()

    barrier = pltpu.get_barrier_semaphore()
    peers = [place(lax.rem(far + d, line) * 2 + near, core) for d in range(1, line)]
    for peer in peers + [core_mate, near_mate, group_mate, after, before]:
        pl.semaphore_signal(barrier, inc=1, device_id=peer, device_id_type=pl.DeviceIdType.MESH)
    pl.semaphore_wait(barrier, len(peers) + 5)

    def remote(src, dst, send, recv, device):
        return pltpu.make_async_remote_copy(
            src_ref=src, dst_ref=dst, send_sem=send, recv_sem=recv,
            device_id=device, device_id_type=pl.DeviceIdType.MESH,
        )

    def span(which, p):
        return pl.ds(pl.multiple_of(which * half + p * piece, piece), piece)

    def cols(z):
        return pl.ds(pl.multiple_of(z * width, width), width)

    loads[0].wait()
    loads[1].wait()
    tail[...] = (
        k_buf[rows - block :, :].astype(jnp.float32) * v_buf[rows - block :, :].astype(jnp.float32)
    ).astype(jnp.bfloat16)
    edge = remote(tail, halo, halo_sem.at[0], halo_sem.at[1], after)
    first, last = linear == 0, linear == seq_count * 2 - 1

    @pl.when(jnp.logical_not(last))
    def _():
        edge.start()

    @pl.when(first)
    def _():
        halo[...] = jnp.zeros_like(halo)


    def source(d):
        return lax.rem(far + line - d, line)

    def along_z(src, dst, send, d, p, step):
        return remote(src, dst, send, zrecv.at[d - 1, p], place((far + step) * 2 + near, core))

    def own_right(p):
        return along_z(w_hbm.at[span(group, p), :], w_full.at[span(group, p), cols(far)], hsend.at[0, p], 1, p, 1)

    def own_left(p):
        return along_z(w_hbm.at[span(group, p), :], w_full.at[span(group, p), cols(far)], hsend.at[1, p], line - 1, p, -1)

    def onward(d, p, step):
        part = w_full.at[span(group, p), cols(source(d))]
        return along_z(part, part, zsend.at[d - 1, p], d + step, p, step)

    def across(d, p, which):
        part = w_full.at[span(which, p), cols(source(d))]
        return remote(part, part, ysend.at[d - 1, p], yrecv.at[d - 1, p], group_mate)

    order = [sorted(range(1, line), key=lambda d, z=z: d if d <= z else line - d) for z in range(line)]

    def nth(k):
        return sum((far == z).astype(jnp.int32) * order[z][k] for z in range(line))

    def goes_right(d):
        return (far >= d) & (far < line - 1)

    def goes_left(d):
        return (far < d) & (far > 0)

    def hand_on(k, p):
        d = nth(k)
        part = w_full.at[span(group, p), cols(source(d))]
        remote(part, part, zsend.at[d - 1, p], zrecv.at[d - 1, p], group_mate).wait_recv()

        @pl.when(goes_right(d))
        def _():
            onward(d, p, 1).start()

        @pl.when(goes_left(d))
        def _():
            onward(d, p, -1).start()

        across(d, p, group).start()

    for p in range(PIECES):
        @pl.when(far < line - 1)
        def _():
            own_right(p).start()

        @pl.when(far > 0)
        def _():
            own_left(p).start()

    loads[2].wait()

    @pl.when(jnp.logical_not(last))
    def _():
        edge.wait_send()

    @pl.when(jnp.logical_not(first))
    def _():
        edge.wait_recv()

    groups_per_tile = LANES // per_group
    lane_group = lax.broadcasted_iota(jnp.int32, (block, 2 * LANES), 1) % LANES // per_group
    my_rows = pl.ds(pl.multiple_of(me * rows, rows), rows)

    def tile(t, carry):
        lanes = pl.ds(pl.multiple_of(t * LANES, LANES), LANES)
        product = (k_buf[:, lanes].astype(jnp.float32) * v_buf[:, lanes].astype(jnp.float32)).astype(jnp.bfloat16)
        past = halo[:, lanes]
        upper, lower = product[:block], product[block:]
        window = jnp.concatenate(
            [jnp.concatenate([past, upper], axis=1), jnp.concatenate([upper, lower], axis=1)], axis=0
        )
        taps = pattern_ref[pl.ds(pl.multiple_of(t * groups_per_tile, groups_per_tile), groups_per_tile), :]
        matrices = []
        for g in range(groups_per_tile):
            row = jnp.broadcast_to(taps[g : g + 1, :], (block, 2 * block))
            matrices.append(pltpu.roll(row, 0, 1, stride=1, stride_axis=0).astype(jnp.bfloat16))
        every = jnp.dot(jnp.concatenate(matrices, axis=0), window, preferred_element_type=jnp.float32)
        total = every[:block]
        for g in range(1, groups_per_tile):
            total = jnp.where(lane_group == g, every[g * block : (g + 1) * block], total)
        convolved = jnp.concatenate([total[:, :LANES], total[:, LANES:]], axis=0)
        g_buf[my_rows, lanes] = (
            q_buf[:, lanes].astype(jnp.float32)
            * (convolved + skip_ref[:, lanes] * product.astype(jnp.float32))
        ).astype(jnp.bfloat16)
        return carry

    def slot(index, j):
        return g_buf.at[pl.ds(pl.multiple_of(index * rows, rows), rows), j * chunk : (j + 1) * chunk]

    def to_near(j):
        return remote(slot(me, j), slot(me, j), xsend.at[j], xrecv.at[j], near_mate)

    def to_core(j):
        return remote(slot(me, j), slot(me, j), csend.at[j], crecv.at[j], core_mate)

    def pass_on(j):
        part = slot((1 - near) * 2 + core, j)
        return remote(part, part, fsend.at[j], frecv.at[j], core_mate)

    inner = (far > 0) & (far < line - 1)
    tiles = chunk // LANES
    for j in range(PIECES):
        lax.fori_loop(j * tiles, (j + 1) * tiles, tile, 0)
        to_near(j).start()
        to_core(j).start()
        hand_on(0, j)

        @pl.when(inner)
        def _():
            hand_on(1, j)

    def relay(j):
        to_near(j).wait_recv()
        pass_on(j).start()

    for p in range(PIECES):
        @pl.when(inner)
        def _():
            hand_on(2, p)

        @pl.when(jnp.logical_not(inner))
        def _():
            hand_on(1, p)

        if p % 2:
            relay(p // 2)
    keep.wait()

    def other(m):
        return (1 - near if m >= 2 else near), (1 - core if m % 2 else core)

    def give(m, k):
        n, c = other(m)
        return remote(
            leaving.at[m - 1, k], arriving.at[m - 1, k], osend.at[m - 1, k], orecv.at[m - 1, k], place(far * 2 + n, c)
        )

    def strip(k):
        return cols(source(nth(k)) if k < line - 1 else far)

    def finish(k):
        if k < line - 1:
            for p in range(PIECES):
                across(nth(k), p, 1 - group).wait_recv()
        load = pltpu.make_async_copy(w_full.at[:, strip(k)], w_buf, local_sem.at[1])
        load.start()
        load.wait()

        def rows_of(r, carry):
            at = pl.ds(pl.multiple_of(r * rows, rows), rows)
            total_buf[at, strip(k)] = jnp.dot(g_buf[at, :], w_buf[...], preferred_element_type=jnp.float32)
            return carry

        lax.fori_loop(0, 4, rows_of, 0)
        for m in (3, 2, 1):
            n, c = other(m)
            at = pl.ds(pl.multiple_of((n * 2 + c) * rows, rows), rows)
            leaving[m - 1, k] = total_buf[at, strip(k)].astype(jnp.bfloat16)
            give(m, k).start()

    for p in range(PIECES):
        @pl.when(jnp.logical_not(inner))
        def _():
            hand_on(2, p)

        if p < PIECES // 2:
            relay(PIECES // 2 + p)
        elif p == PIECES // 2:
            for j in range(PIECES):
                to_core(j).wait_recv()
                pass_on(j).wait_recv()
            finish(line - 1)
        elif p == PIECES // 2 + 1:
            finish(0)
        elif p == PIECES // 2 + 2:
            finish(1)
    finish(2)

    for k in (3, 0, 1, 2):
        z = source(nth(k)) if k < line - 1 else far
        for m in (0, 1, 2, 3):
            n, c = other(m)
            if m:
                give(m, k).wait()
            at = pl.ds(pl.multiple_of((z * 4 + n * 2 + c) * width, width), width)
            part = arriving[m - 1, k].astype(jnp.float32) if m else total_buf[my_rows, strip(k)]
            out_ref[:, at] = (res_ref[:, at].astype(jnp.float32) + part).astype(jnp.bfloat16)

    for p in range(PIECES):
        to_near(p).wait_send()
        to_core(p).wait_send()
        pass_on(p).wait_send()

        @pl.when(far < line - 1)
        def _():
            own_right(p).wait_send()

        @pl.when(far > 0)
        def _():
            own_left(p).wait_send()

        for d in range(1, line):
            @pl.when(goes_right(d) | goes_left(d))
            def _():
                part = w_full.at[span(group, p), cols(source(d))]
                remote(part, part, zsend.at[d - 1, p], zrecv.at[d - 1, p], group_mate).wait_send()

            across(d, p, group).wait_send()


def tiled_body(mesh, queries, key_proj, value_proj, filter_taps, skip_gain, out_weight, residual):
    rows, channels = queries.shape
    groups_here, block = filter_taps.shape
    depth, width = out_weight.shape
    seq_count = mesh.shape["seq"]
    line = seq_count // 2
    pattern = jnp.pad(filter_taps.astype(jnp.float32)[:, ::-1], ((0, 0), (1, block - 1)))
    hbm = pl.BlockSpec(memory_space=pl.ANY)
    vmem = pl.BlockSpec(memory_space=pltpu.VMEM)
    dma = pltpu.SemaphoreType.DMA
    bf16 = jnp.bfloat16
    out, _ = pl.pallas_call(
        functools.partial(mixer_kernel, seq_count, channels // groups_here),
        out_shape=(
            jax.ShapeDtypeStruct(residual.shape, bf16),
            jax.ShapeDtypeStruct((depth, line * width), bf16),
        ),
        in_specs=[hbm, hbm, hbm, vmem, vmem, hbm, vmem],
        out_specs=(vmem, hbm),
        scratch_shapes=[pltpu.VMEM((rows, channels), bf16)] * 3
        + [pltpu.VMEM((4 * rows, channels), bf16)]
        + [pltpu.VMEM((block, channels), bf16)] * 2
        + [pltpu.VMEM((4 * rows, line * width), jnp.float32), pltpu.VMEM((depth, width), bf16)]
        + [pltpu.VMEM((3, line, rows, width), bf16)] * 2
        + [dma((3,)), dma((2,)), dma((2,)), dma((2, PIECES))]
        + [dma((line - 1, PIECES))] * 4
        + [dma((PIECES,))] * 6
        + [dma((3, line))] * 2,
        compiler_params=pltpu.CompilerParams(
            collective_id=0, has_side_effects=True, vmem_limit_bytes=60 * 2**20
        ),
    )(queries, key_proj, value_proj, pattern, skip_gain[None, :], out_weight, residual)
    return out


def choose(mesh, *args):
    rows, channels = args[0].shape
    groups_here, block = args[3].shape
    if (
        mesh.shape["chan"] == 1 and mesh.shape["groups"] == 2 and mesh.shape["section"] == 2
        and mesh.shape["seq"] % 2 == 0 and mesh.shape["seq"] == 8
        and block == LANES and rows == 2 * block and channels // groups_here * 8 == LANES
    ):
        return tiled_body(mesh, *args)
    return body(*args)


def solution(mesh):
    return jax.shard_map(
        functools.partial(choose, mesh),
        mesh=mesh,
        in_specs=(
            P(("groups", "seq", "section"), "chan"),
            P(("groups", "seq", "section"), "chan"),
            P(("groups", "seq", "section"), "chan"),
            P("chan", None),
            P("chan"),
            P("chan", ("seq", "section")),
            P(("groups", "seq", "section"), "chan"),
        ),
        out_specs=P(("groups", "seq", "section"), "chan"),
        check_vma=False,
    )
```
